32 devices in a mesh: pipe: 8 (over z, y), head: 4 (over x, core).
Axes of the slice: x: 2, y: 2, z: 4, core: 2. Of those that a mesh axis runs over, the one named last changes fastest.
Arguments:
- queries: bfloat16 [2, 2048, 8192], P(None, 'pipe', 'head'), may hold values from -150 to 150
- keys: bfloat16 [2048, 1024], P(('pipe', 'head')), may hold values from -7 to 7
- values: bfloat16 [2048, 1024], P(('pipe', 'head')), may hold values from -6 to 6
- slice_index: int32 [2, 8], replicated, may hold values from 0 to 7, each once within a row
Outputs:
- attended: bfloat16 [2, 2048, 8192], P(None, 'pipe', 'head')
The draws below stay inside these ranges and needn't reach their ends.
Inputs may be any that keep to these rules, and one draw needn't show every extreme that they name: Each row of slice_index is a permutation of 0 to 7.
All inputs are finite; a program needn't handle non-finite values.
Results may differ from the reference program's by a relative error of at most 0.0041.
Values may be sent and summed in bfloat16 or wider, within the bound.
A program may use at most 128 MiB of HBM per device.

```python
import jax
import jax.numpy as jnp
from jax import lax

QUERY_HEADS = 64
KEY_VALUE_HEADS = 8
HEAD_SIZE = 128
SLICE_ROWS = 256
TICK_COUNT = 2
SEQUENCE_TOKENS = 2048
N_PIPE = 8


def key_region(key):
    query_field = jax.random.truncated_normal(jax.random.fold_in(key, 11), -6.0, 6.0, (SEQUENCE_TOKENS, KEY_VALUE_HEADS * HEAD_SIZE), jnp.float32)
    return query_field


def draw_keys(key, part):
    return key_region(key).astype(jnp.bfloat16)


def draw_queries(key, part):
    query_field = jax.random.truncated_normal(jax.random.fold_in(key, 21), -6.0, 6.0, (TICK_COUNT, SEQUENCE_TOKENS, QUERY_HEADS * HEAD_SIZE), jnp.float32)
    return query_field.astype(jnp.bfloat16)


def levels(rng, shape, split, least, largest):
    loudness, own = 1.0, jax.random.fold_in(rng, 6)
    for axis_at, shards_of in split:
        draws = jnp.exp(jax.random.uniform(jax.random.fold_in(own, axis_at), (shards_of,), jnp.float32, least / len(split), largest / len(split)))
        loudness = loudness * jnp.repeat(draws, shape[axis_at] // shards_of).reshape([-1 if axis == axis_at else 1 for axis in range(len(shape))])
    return loudness


def centred(own_key, shape, width, reach, shards=(), kind=jnp.bfloat16):
    result = width * jax.random.normal(own_key, shape, jnp.float32)
    if shards:
        result = result * levels(own_key, shape, shards, -0.22, 0.18)
    return jnp.clip(result, -reach, reach).astype(kind)


def setup_inputs(seed: int = 0) -> dict:
    seeds = jax.random.split(jax.random.key(seed), 5)
    return {
        "queries": draw_queries(jax.random.fold_in(seeds[4], 71), 0),
        "keys": draw_keys(jax.random.fold_in(seeds[4], 71), 0),
        "values": centred(seeds[2], (SEQUENCE_TOKENS, KEY_VALUE_HEADS * HEAD_SIZE), 1.0, 6.0, ((0, 32),)),
        "slice_index": jax.vmap(lambda own: jax.random.permutation(own, N_PIPE))(jax.random.split(seeds[3], TICK_COUNT)).reshape((TICK_COUNT, N_PIPE)).astype(jnp.int32),
    }


NEG = -1.0e30


def reference(queries, keys, values, slice_index):
    query_group = QUERY_HEADS // KEY_VALUE_HEADS
    query_matrix = queries.reshape(TICK_COUNT, N_PIPE, SLICE_ROWS, KEY_VALUE_HEADS, query_group, HEAD_SIZE)
    key_matrix = keys.reshape(SEQUENCE_TOKENS, KEY_VALUE_HEADS, HEAD_SIZE)
    value_matrix = values.reshape(SEQUENCE_TOKENS, KEY_VALUE_HEADS, HEAD_SIZE)
    key_pos = jnp.arange(SEQUENCE_TOKENS, dtype=jnp.int32)

    def single_output(item_index):
        tick_index = item_index // (N_PIPE * KEY_VALUE_HEADS)
        section_index = (item_index // KEY_VALUE_HEADS) % N_PIPE
        head_index = item_index % KEY_VALUE_HEADS
        query = query_matrix[tick_index, section_index, :, head_index].astype(jnp.float32)
        key_head = key_matrix[:, head_index].astype(jnp.float32)
        value_head = value_matrix[:, head_index].astype(jnp.float32)
        query_pos = slice_index[tick_index, section_index].astype(jnp.int32) * SLICE_ROWS + jnp.arange(SLICE_ROWS, dtype=jnp.int32)
        scores = jnp.einsum("rgd,kd->rgk", query, key_head) * (HEAD_SIZE ** -0.5)
        allowed = (key_pos[None, :] <= query_pos[:, None])[:, None, :]
        peak = jnp.max(jnp.where(allowed, scores, NEG), axis=-1)
        weights = jnp.where(allowed, jnp.exp(scores - peak[..., None]), 0.0)
        total = jnp.sum(weights, axis=-1)
        numer = jnp.einsum("rgk,kd->rgd", weights.astype(jnp.bfloat16).astype(jnp.float32), value_head)
        return (numer / total[..., None]).astype(jnp.bfloat16)

    output_list = lax.map(single_output, jnp.arange(TICK_COUNT * N_PIPE * KEY_VALUE_HEADS, dtype=jnp.int32))
    output_list = output_list.reshape(TICK_COUNT, N_PIPE, KEY_VALUE_HEADS, SLICE_ROWS, query_group, HEAD_SIZE).transpose(0, 1, 3, 2, 4, 5)
    return output_list.reshape(TICK_COUNT, SEQUENCE_TOKENS, QUERY_HEADS * HEAD_SIZE)
```

```python
import math

import jax
import jax.numpy as jnp
from jax import lax
from jax.experimental import pallas as pl
from jax.experimental.pallas import tpu as pltpu
from jax.sharding import PartitionSpec as P

HEAD_SIZE = 128
NEG = -1e30
TO_EXP2 = HEAD_SIZE ** (-0.5) * math.log2(math.e)
SUPER = 8
UNROLL = 2


def scores_of(query, key_block):
    return lax.dot_general(query, key_block, (((1,), (1,)), ((), ())), preferred_element_type=jnp.float32)


def weigh(scores, peak, value_block):
    weights = jnp.exp2((scores - peak) * TO_EXP2).astype(jnp.bfloat16)
    ones = jnp.ones(value_block.shape, jnp.bfloat16)
    return jnp.dot(weights, jnp.concatenate([value_block, ones], axis=1), preferred_element_type=jnp.float32)


def attend_kernel(slices, group, index_ref, q_ref, k_ref, v_ref, o_ref, best_ref, accum_ref):
    tick = pl.program_id(1)
    rows = q_ref.shape[1]
    mine = index_ref[tick]
    full = mine // SUPER
    rest = lax.rem(mine, SUPER) + 1
    several = slices > SUPER
    if several:
        best_ref[...] = jnp.full(best_ref.shape, NEG, jnp.float32)
        accum_ref[...] = jnp.zeros(accum_ref.shape, jnp.float32)

        @pl.loop(0, full)
        def _(step):
            at = pl.ds(pl.multiple_of(step * (SUPER * rows), SUPER * rows), SUPER * rows)

            @pl.loop(0, group)
            def _(g):
                query = q_ref[0, :, pl.ds(pl.multiple_of(g * HEAD_SIZE, HEAD_SIZE), HEAD_SIZE)]
                scores = scores_of(query, k_ref[at, :])
                before = best_ref[g]
                peak = jnp.maximum(before, jnp.max(scores, axis=-1, keepdims=True))
                best_ref[g] = peak
                accum_ref[g] = accum_ref[g] * jnp.exp2((before - peak) * TO_EXP2) + weigh(scores, peak, v_ref[at, :])

    low = lax.broadcasted_iota(jnp.int32, (rows, rows), 0) >= lax.broadcasted_iota(jnp.int32, (rows, rows), 1)
    for extent in range(1, min(SUPER, slices) + 1):

        @pl.when(rest == extent)
        def _(extent=extent):
            start = full * (SUPER * rows) if several else 0

            def one(g):
                columns = pl.ds(pl.multiple_of(g * HEAD_SIZE, HEAD_SIZE), HEAD_SIZE)
                query = q_ref[0, :, columns]
                at = pl.ds(pl.multiple_of(start, SUPER * rows), extent * rows) if several else pl.ds(0, extent * rows)
                scores = scores_of(query, k_ref[at, :])
                edge = jnp.where(low, scores[:, (extent - 1) * rows:], NEG)
                scores = jnp.concatenate([scores[:, :(extent - 1) * rows], edge], axis=1) if extent > 1 else edge
                peak = jnp.max(scores, axis=-1, keepdims=True)
                if several:
                    peak = jnp.maximum(peak, best_ref[g])
                result = weigh(scores, peak, v_ref[at, :])
                if several:
                    result = result + accum_ref[g] * jnp.exp2((best_ref[g] - peak) * TO_EXP2)
                o_ref[0, :, columns] = (result[:, :HEAD_SIZE] / result[:, HEAD_SIZE:]).astype(o_ref.dtype)

            @pl.loop(0, group // UNROLL)
            def _(step):
                for u in range(UNROLL):
                    one(step * UNROLL + u)


def attend(queries, key_all, value_all, index):
    ticks, rows, columns = queries.shape
    extent, width = key_all.shape
    heads = width // HEAD_SIZE
    group = columns // width
    slices = extent // rows
    state = group if slices > SUPER else 1
    return pl.pallas_call(
        lambda *refs: attend_kernel(slices, group, *refs),
        out_shape=jax.ShapeDtypeStruct(queries.shape, queries.dtype),
        grid_spec=pltpu.PrefetchScalarGridSpec(
            num_scalar_prefetch=1,
            grid=(heads, ticks),
            in_specs=[
                pl.BlockSpec((1, rows, group * HEAD_SIZE), lambda h, t, _: (t, 0, h)),
                pl.BlockSpec((extent, HEAD_SIZE), lambda h, t, _: (0, h)),
                pl.BlockSpec((extent, HEAD_SIZE), lambda h, t, _: (0, h)),
            ],
            out_specs=pl.BlockSpec((1, rows, group * HEAD_SIZE), lambda h, t, _: (t, 0, h)),
            scratch_shapes=[
                pltpu.VMEM((state, rows, 1), jnp.float32),
                pltpu.VMEM((state, rows, 2 * HEAD_SIZE), jnp.float32),
            ],
        ),
        compiler_params=pltpu.CompilerParams(vmem_limit_bytes=60 * 2 ** 20),
        name="attend",
    )(index, queries, key_all, value_all)


def on_device(queries, keys, values, slice_index):
    key_cols = lax.all_to_all(keys, "head", split_axis=1, concat_axis=0, tiled=True)
    value_cols = lax.all_to_all(values, "head", split_axis=1, concat_axis=0, tiled=True)
    key_all = lax.all_gather(key_cols, "pipe", axis=0, tiled=True)
    value_all = lax.all_gather(value_cols, "pipe", axis=0, tiled=True)
    index = lax.dynamic_index_in_dim(slice_index, lax.axis_index("pipe"), axis=1, keepdims=False)
    return attend(queries, key_all, value_all, index)


def solution(mesh):
    return jax.shard_map(
        on_device,
        mesh=mesh,
        in_specs=(
            P(None, "pipe", "head"),
            P(("pipe", "head"), None),
            P(("pipe", "head"), None),
            P(),
        ),
        out_specs=P(None, "pipe", "head"),
        check_vma=False,
    )
```

```python
import math

import jax
import jax.numpy as jnp
from jax import lax
from jax.experimental import pallas as pl
from jax.experimental.pallas import tpu as pltpu
from jax.sharding import PartitionSpec as P

HEAD_SIZE = 128
NEG = -1e30
TO_EXP2 = HEAD_SIZE ** (-0.5) * math.log2(math.e)
SUPER = 8
UNROLL = 2


def scores_of(query, key_block):
    return lax.dot_general(query, key_block, (((1,), (1,)), ((), ())), preferred_element_type=jnp.float32)


def weigh(scores, peak, value_block):
    weights = jnp.exp2((scores - peak) * TO_EXP2).astype(jnp.bfloat16)
    ones = jnp.ones(value_block.shape, jnp.bfloat16)
    return jnp.dot(weights, jnp.concatenate([value_block, ones], axis=1), preferred_element_type=jnp.float32)


def attend_kernel(slices, group, index_ref, q_ref, k_ref, v_ref, o_ref, best_ref, accum_ref):
    tick = pl.program_id(1)
    rows = q_ref.shape[1]
    mine = index_ref[tick]
    full = mine // SUPER
    rest = lax.rem(mine, SUPER) + 1
    several = slices > SUPER
    if several:
        best_ref[...] = jnp.full(best_ref.shape, NEG, jnp.float32)
        accum_ref[...] = jnp.zeros(accum_ref.shape, jnp.float32)

        @pl.loop(0, full)
        def _(step):
            at = pl.ds(pl.multiple_of(step * (SUPER * rows), SUPER * rows), SUPER * rows)

            @pl.loop(0, group)
            def _(g):
                query = q_ref[0, :, pl.ds(pl.multiple_of(g * HEAD_SIZE, HEAD_SIZE), HEAD_SIZE)]
                scores = scores_of(query, k_ref[at, :])
                before = best_ref[g]
                peak = jnp.maximum(before, jnp.max(scores, axis=-1, keepdims=True))
                best_ref[g] = peak
                accum_ref[g] = accum_ref[g] * jnp.exp2((before - peak) * TO_EXP2) + weigh(scores, peak, v_ref[at, :])

    low = lax.broadcasted_iota(jnp.int32, (rows, rows), 0) >= lax.broadcasted_iota(jnp.int32, (rows, rows), 1)
    for extent in range(1, min(SUPER, slices) + 1):

        @pl.when(rest == extent)
        def _(extent=extent):
            start = full * (SUPER * rows) if several else 0

            def one(g):
                columns = pl.ds(pl.multiple_of(g * HEAD_SIZE, HEAD_SIZE), HEAD_SIZE)
                query = q_ref[0, :, columns]
                at = pl.ds(pl.multiple_of(start, SUPER * rows), extent * rows) if several else pl.ds(0, extent * rows)
                scores = scores_of(query, k_ref[at, :])
                edge = jnp.where(low, scores[:, (extent - 1) * rows:], NEG)
                scores = jnp.concatenate([scores[:, :(extent - 1) * rows], edge], axis=1) if extent > 1 else edge
                peak = jnp.max(scores, axis=-1, keepdims=True)
                if several:
                    peak = jnp.maximum(peak, best_ref[g])
                result = weigh(scores, peak, v_ref[at, :])
                if several:
                    result = result + accum_ref[g] * jnp.exp2((best_ref[g] - peak) * TO_EXP2)
                o_ref[0, :, columns] = (result[:, :HEAD_SIZE] / result[:, HEAD_SIZE:]).astype(o_ref.dtype)

            @pl.loop(0, group // UNROLL)
            def _(step):
                for u in range(UNROLL):
                    one(step * UNROLL + u)


def attend(queries, key_all, value_all, index):
    ticks, rows, columns = queries.shape
    extent, width = key_all.shape
    heads = width // HEAD_SIZE
    group = columns // width
    slices = extent // rows
    state = group if slices > SUPER else 1
    return pl.pallas_call(
        lambda *refs: attend_kernel(slices, group, *refs),
        out_shape=jax.ShapeDtypeStruct(queries.shape, queries.dtype),
        grid_spec=pltpu.PrefetchScalarGridSpec(
            num_scalar_prefetch=1,
            grid=(heads, ticks),
            in_specs=[
                pl.BlockSpec((1, rows, group * HEAD_SIZE), lambda h, t, _: (t, 0, h)),
                pl.BlockSpec((extent, HEAD_SIZE), lambda h, t, _: (0, h)),
                pl.BlockSpec((extent, HEAD_SIZE), lambda h, t, _: (0, h)),
            ],
            out_specs=pl.BlockSpec((1, rows, group * HEAD_SIZE), lambda h, t, _: (t, 0, h)),
            scratch_shapes=[
                pltpu.VMEM((state, rows, 1), jnp.float32),
                pltpu.VMEM((state, rows, 2 * HEAD_SIZE), jnp.float32),
            ],
        ),
        compiler_params=pltpu.CompilerParams(vmem_limit_bytes=60 * 2 ** 20),
        name="attend",
    )(index, queries, key_all, value_all)


MESH = pl.DeviceIdType.MESH


def gather_kernel(n_pipe, n_head, k_ref, v_ref, ko_ref, vo_ref, kbuf, vbuf, local_sem, head_send, head_recv, left_send, right_send, side_send, chunk_recv, out_sem):
    me = lax.axis_index("pipe")
    head = lax.axis_index("head")
    side = me + 1 - 2 * lax.rem(me, 2)
    row = lax.div(me, 2)
    line = n_pipe // 2
    has_left, has_right = row > 0, row < line - 1
    piece = k_ref.shape[0]
    rows = piece * n_head
    width = kbuf.shape[1]
    ins, bufs, outs = (k_ref, v_ref), (kbuf, vbuf), (ko_ref, vo_ref)

    barrier = pltpu.get_barrier_semaphore()
    for other in range(1, n_head):
        pl.semaphore_signal(barrier, inc=1, device_id=(me, lax.rem(head + other, n_head)), device_id_type=MESH)
    pl.semaphore_signal(barrier, inc=1, device_id=(side, head), device_id_type=MESH)

    @pl.when(has_left)
    def _():
        pl.semaphore_signal(barrier, inc=1, device_id=(me - 2, head), device_id_type=MESH)

    @pl.when(has_right)
    def _():
        pl.semaphore_signal(barrier, inc=1, device_id=(me + 2, head), device_id_type=MESH)

    pl.semaphore_wait(barrier, n_head + jnp.where(has_left, 1, 0) + jnp.where(has_right, 1, 0))

    def chunk(kind, owner):
        return bufs[kind].at[pl.ds(pl.multiple_of(owner * rows, rows), rows), :]

    def spot(kind, source):
        return bufs[kind].at[pl.ds(pl.multiple_of(me * rows + source * piece, piece), piece), :]

    def columns(kind, target):
        return ins[kind].at[:, pl.ds(pl.multiple_of(target * width, width), width)]

    def exchange(kind, other):
        return pltpu.make_async_remote_copy(
            columns(kind, lax.rem(head + other, n_head)), spot(kind, head),
            head_send.at[kind, other], head_recv.at[kind, other],
            device_id=(me, lax.rem(head + other, n_head)), device_id_type=MESH)

    def arrival(kind, other):
        source = lax.rem(head + n_head - other, n_head)
        return pltpu.make_async_remote_copy(
            columns(kind, head), spot(kind, source),
            head_send.at[kind, other], head_recv.at[kind, other],
            device_id=(me, source), device_id_type=MESH)

    def pass_on(kind, owner, target, sems):
        return pltpu.make_async_remote_copy(
            chunk(kind, owner), chunk(kind, owner), sems.at[kind, owner], chunk_recv.at[kind, owner],
            device_id=(target, head), device_id_type=MESH)

    def to_left(kind, owner):
        return pass_on(kind, owner, me - 2, left_send)

    def to_right(kind, owner):
        return pass_on(kind, owner, me + 2, right_send)

    def to_side(kind, owner):
        return pass_on(kind, owner, side, side_send)

    def write(kind, owner):
        at = pl.ds(pl.multiple_of(owner * rows, rows), rows)
        return pltpu.make_async_copy(bufs[kind].at[at, :], outs[kind].at[at, :], out_sem.at[kind, owner])

    for kind in range(2):
        for other in range(1, n_head):
            exchange(kind, other).start()
        pltpu.make_async_copy(columns(kind, head), spot(kind, head), local_sem.at[kind]).start()
    for kind in range(2):
        pltpu.make_async_copy(columns(kind, head), spot(kind, head), local_sem.at[kind]).wait()
        for other in range(1, n_head):
            arrival(kind, other).wait_recv()
        to_side(kind, me).start()

        @pl.when(has_left)
        def _():
            to_left(kind, me).start()

        @pl.when(has_right)
        def _():
            to_right(kind, me).start()

        write(kind, me).start()

    @pl.loop(1, line)
    def _(step):
        for kind in range(2):

            @pl.when(row >= step)
            def _():
                owner = me - 2 * step
                to_right(kind, owner).wait_recv()
                to_side(kind, owner).start()

                @pl.when(has_right)
                def _():
                    to_right(kind, owner).start()

                write(kind, owner).start()

            @pl.when(row + step < line)
            def _():
                owner = me + 2 * step
                to_left(kind, owner).wait_recv()
                to_side(kind, owner).start()

                @pl.when(has_left)
                def _():
                    to_left(kind, owner).start()

                write(kind, owner).start()

    @pl.loop(0, line)
    def _(index):
        for kind in range(2):
            owner = 2 * index + lax.rem(side, 2)
            to_side(kind, owner).wait_recv()
            write(kind, owner).start()

    for kind in range(2):
        for other in range(1, n_head):
            exchange(kind, other).wait_send()

    @pl.loop(0, line)
    def _(index):
        for kind in range(2):
            owner = 2 * index + lax.rem(me, 2)
            to_side(kind, owner).wait_send()

            @pl.when(jnp.logical_and(has_right, index <= row))
            def _():
                to_right(kind, owner).wait_send()

            @pl.when(jnp.logical_and(has_left, index >= row))
            def _():
                to_left(kind, owner).wait_send()

    @pl.loop(0, n_pipe)
    def _(owner):
        for kind in range(2):
            write(kind, owner).wait()


def gather(keys, values, n_pipe, n_head):
    piece, columns = keys.shape
    shape = (piece * n_head * n_pipe, columns // n_head)
    whole = pl.BlockSpec(memory_space=pltpu.VMEM)
    dma = pltpu.SemaphoreType.DMA
    return pl.pallas_call(
        lambda *refs: gather_kernel(n_pipe, n_head, *refs),
        out_shape=[jax.ShapeDtypeStruct(shape, keys.dtype)] * 2,
        in_specs=[whole, whole],
        out_specs=[pl.BlockSpec(memory_space=pl.ANY)] * 2,
        scratch_shapes=[
            pltpu.VMEM(shape, keys.dtype),
            pltpu.VMEM(shape, keys.dtype),
            dma((2,)),
            dma((2, n_head)),
            dma((2, n_head)),
            dma((2, n_pipe)),
            dma((2, n_pipe)),
            dma((2, n_pipe)),
            dma((2, n_pipe)),
            dma((2, n_pipe)),
        ],
        compiler_params=pltpu.CompilerParams(collective_id=0, has_side_effects=True, vmem_limit_bytes=60 * 2 ** 20),
        name="gather",
    )(keys, values)


def on_device(sizes, queries, keys, values, slice_index):
    key_all, value_all = gather(keys, values, *sizes)
    index = lax.dynamic_index_in_dim(slice_index, lax.axis_index("pipe"), axis=1, keepdims=False)
    return attend(queries, key_all, value_all, index)


def solution(mesh):
    sizes = (mesh.shape["pipe"], mesh.shape["head"])
    return jax.shard_map(
        lambda *arrays: on_device(sizes, *arrays),
        mesh=mesh,
        in_specs=(
            P(None, "pipe", "head"),
            P(("pipe", "head"), None),
            P(("pipe", "head"), None),
            P(),
        ),
        out_specs=P(None, "pipe", "head"),
        check_vma=False,
    )
```

```python
import math

import jax
import jax.numpy as jnp
from jax import lax
from jax.experimental import pallas as pl
from jax.experimental.pallas import tpu as pltpu
from jax.sharding import PartitionSpec as P

HEAD_SIZE = 128
NEG = -1e30
TO_EXP2 = HEAD_SIZE ** (-0.5) * math.log2(math.e)
SUPER = 8
UNROLL = 4


def scores_of(query, key_block):
    return lax.dot_general(query, key_block, (((1,), (1,)), ((), ())), preferred_element_type=jnp.float32)


def weigh(scores, peak, value_block):
    weights = jnp.exp2((scores - peak) * TO_EXP2).astype(jnp.bfloat16)
    ones = jnp.ones(value_block.shape, jnp.bfloat16)
    return jnp.dot(weights, jnp.concatenate([value_block, ones], axis=1), preferred_element_type=jnp.float32)


def attend_kernel(slices, group, index_ref, q_ref, k_ref, v_ref, o_ref, best_ref, accum_ref):
    tick = pl.program_id(1)
    rows = q_ref.shape[1]
    mine = index_ref[tick]
    full = mine // SUPER
    rest = lax.rem(mine, SUPER) + 1
    several = slices > SUPER
    if several:
        best_ref[...] = jnp.full(best_ref.shape, NEG, jnp.float32)
        accum_ref[...] = jnp.zeros(accum_ref.shape, jnp.float32)

        @pl.loop(0, full)
        def _(step):
            at = pl.ds(pl.multiple_of(step * (SUPER * rows), SUPER * rows), SUPER * rows)

            @pl.loop(0, group)
            def _(g):
                query = q_ref[0, :, pl.ds(pl.multiple_of(g * HEAD_SIZE, HEAD_SIZE), HEAD_SIZE)]
                scores = scores_of(query, k_ref[at, :])
                before = best_ref[g]
                peak = jnp.maximum(before, jnp.max(scores, axis=-1, keepdims=True))
                best_ref[g] = peak
                accum_ref[g] = accum_ref[g] * jnp.exp2((before - peak) * TO_EXP2) + weigh(scores, peak, v_ref[at, :])

    low = lax.broadcasted_iota(jnp.int32, (rows, rows), 0) >= lax.broadcasted_iota(jnp.int32, (rows, rows), 1)
    for extent in range(1, min(SUPER, slices) + 1):

        @pl.when(rest == extent)
        def _(extent=extent):
            start = full * (SUPER * rows) if several else 0

            def one(g):
                columns = pl.ds(pl.multiple_of(g * HEAD_SIZE, HEAD_SIZE), HEAD_SIZE)
                query = q_ref[0, :, columns]
                at = pl.ds(pl.multiple_of(start, SUPER * rows), extent * rows) if several else pl.ds(0, extent * rows)
                scores = scores_of(query, k_ref[at, :])
                edge = jnp.where(low, scores[:, (extent - 1) * rows:], NEG)
                scores = jnp.concatenate([scores[:, :(extent - 1) * rows], edge], axis=1) if extent > 1 else edge
                peak = jnp.max(scores, axis=-1, keepdims=True)
                if several:
                    peak = jnp.maximum(peak, best_ref[g])
                result = weigh(scores, peak, v_ref[at, :])
                if several:
                    result = result + accum_ref[g] * jnp.exp2((best_ref[g] - peak) * TO_EXP2)
                o_ref[0, :, columns] = (result[:, :HEAD_SIZE] / result[:, HEAD_SIZE:]).astype(o_ref.dtype)

            @pl.loop(0, group // UNROLL)
            def _(step):
                for u in range(UNROLL):
                    one(step * UNROLL + u)


def attend(queries, key_all, value_all, index):
    ticks, rows, columns = queries.shape
    extent, width = key_all.shape
    heads = width // HEAD_SIZE
    group = columns // width
    slices = extent // rows
    state = group if slices > SUPER else 1
    return pl.pallas_call(
        lambda *refs: attend_kernel(slices, group, *refs),
        out_shape=jax.ShapeDtypeStruct(queries.shape, queries.dtype),
        grid_spec=pltpu.PrefetchScalarGridSpec(
            num_scalar_prefetch=1,
            grid=(heads, ticks),
            in_specs=[
                pl.BlockSpec((1, rows, group * HEAD_SIZE), lambda h, t, _: (t, 0, h)),
                pl.BlockSpec((extent, HEAD_SIZE), lambda h, t, _: (0, h)),
                pl.BlockSpec((extent, HEAD_SIZE), lambda h, t, _: (0, h)),
            ],
            out_specs=pl.BlockSpec((1, rows, group * HEAD_SIZE), lambda h, t, _: (t, 0, h)),
            scratch_shapes=[
                pltpu.VMEM((state, rows, 1), jnp.float32),
                pltpu.VMEM((state, rows, 2 * HEAD_SIZE), jnp.float32),
            ],
        ),
        compiler_params=pltpu.CompilerParams(vmem_limit_bytes=60 * 2 ** 20),
        name="attend",
    )(index, queries, key_all, value_all)


MESH = pl.DeviceIdType.MESH


def gather_kernel(n_pipe, n_head, k_ref, v_ref, ko_ref, vo_ref, kbuf, vbuf, local_sem, head_send, head_recv, left_send, right_send, side_send, chunk_recv, out_sem):
    me = lax.axis_index("pipe")
    head = lax.axis_index("head")
    side = me + 1 - 2 * lax.rem(me, 2)
    row = lax.div(me, 2)
    line = n_pipe // 2
    has_left, has_right = row > 0, row < line - 1
    piece = k_ref.shape[0]
    rows = piece * n_head
    width = kbuf.shape[1]
    ins, bufs, outs = (k_ref, v_ref), (kbuf, vbuf), (ko_ref, vo_ref)

    barrier = pltpu.get_barrier_semaphore()
    for other in range(1, n_head):
        pl.semaphore_signal(barrier, inc=1, device_id=(me, lax.rem(head + other, n_head)), device_id_type=MESH)
    pl.semaphore_signal(barrier, inc=1, device_id=(side, head), device_id_type=MESH)

    @pl.when(has_left)
    def _():
        pl.semaphore_signal(barrier, inc=1, device_id=(me - 2, head), device_id_type=MESH)

    @pl.when(has_right)
    def _():
        pl.semaphore_signal(barrier, inc=1, device_id=(me + 2, head), device_id_type=MESH)

    pl.semaphore_wait(barrier, n_head + jnp.where(has_left, 1, 0) + jnp.where(has_right, 1, 0))

    def chunk(kind, owner):
        return bufs[kind].at[pl.ds(pl.multiple_of(owner * rows, rows), rows), :]

    def spot(kind, source):
        return bufs[kind].at[pl.ds(pl.multiple_of(me * rows + source * piece, piece), piece), :]

    def columns(kind, target):
        return ins[kind].at[:, pl.ds(pl.multiple_of(target * width, width), width)]

    def exchange(kind, other):
        return pltpu.make_async_remote_copy(
            columns(kind, lax.rem(head + other, n_head)), spot(kind, head),
            head_send.at[kind, other], head_recv.at[kind, other],
            device_id=(me, lax.rem(head + other, n_head)), device_id_type=MESH)

    def arrival(kind, other):
        source = lax.rem(head + n_head - other, n_head)
        return pltpu.make_async_remote_copy(
            columns(kind, head), spot(kind, source),
            head_send.at[kind, other], head_recv.at[kind, other],
            device_id=(me, source), device_id_type=MESH)

    def pass_on(kind, owner, target, sems):
        return pltpu.make_async_remote_copy(
            chunk(kind, owner), chunk(kind, owner), sems.at[kind, owner], chunk_recv.at[kind, owner],
            device_id=(target, head), device_id_type=MESH)

    def to_left(kind, owner):
        return pass_on(kind, owner, me - 2, left_send)

    def to_right(kind, owner):
        return pass_on(kind, owner, me + 2, right_send)

    def to_side(kind, owner):
        return pass_on(kind, owner, side, side_send)

    def write(kind, owner):
        at = pl.ds(pl.multiple_of(owner * rows, rows), rows)
        return pltpu.make_async_copy(bufs[kind].at[at, :], outs[kind].at[at, :], out_sem.at[kind, owner])

    for kind in range(2):
        for other in range(1, n_head):
            exchange(kind, other).start()
        pltpu.make_async_copy(columns(kind, head), spot(kind, head), local_sem.at[kind]).start()
    for kind in range(2):
        pltpu.make_async_copy(columns(kind, head), spot(kind, head), local_sem.at[kind]).wait()
        for other in range(1, n_head):
            arrival(kind, other).wait_recv()
        to_side(kind, me).start()

        @pl.when(has_left)
        def _():
            to_left(kind, me).start()

        @pl.when(has_right)
        def _():
            to_right(kind, me).start()

        write(kind, me).start()

    @pl.loop(1, line)
    def _(step):
        for kind in range(2):

            @pl.when(row >= step)
            def _():
                owner = me - 2 * step
                to_right(kind, owner).wait_recv()
                to_side(kind, owner).start()

                @pl.when(has_right)
                def _():
                    to_right(kind, owner).start()

                write(kind, owner).start()

            @pl.when(row + step < line)
            def _():
                owner = me + 2 * step
                to_left(kind, owner).wait_recv()
                to_side(kind, owner).start()

                @pl.when(has_left)
                def _():
                    to_left(kind, owner).start()

                write(kind, owner).start()

    @pl.loop(0, line)
    def _(index):
        for kind in range(2):
            owner = 2 * index + lax.rem(side, 2)
            to_side(kind, owner).wait_recv()
            write(kind, owner).start()

    for kind in range(2):
        for other in range(1, n_head):
            exchange(kind, other).wait_send()

    @pl.loop(0, line)
    def _(index):
        for kind in range(2):
            owner = 2 * index + lax.rem(me, 2)
            to_side(kind, owner).wait_send()

            @pl.when(jnp.logical_and(has_right, index <= row))
            def _():
                to_right(kind, owner).wait_send()

            @pl.when(jnp.logical_and(has_left, index >= row))
            def _():
                to_left(kind, owner).wait_send()

    @pl.loop(0, n_pipe)
    def _(owner):
        for kind in range(2):
            write(kind, owner).wait()


def gather(keys, values, n_pipe, n_head):
    piece, columns = keys.shape
    shape = (piece * n_head * n_pipe, columns // n_head)
    whole = pl.BlockSpec(memory_space=pltpu.VMEM)
    dma = pltpu.SemaphoreType.DMA
    return pl.pallas_call(
        lambda *refs: gather_kernel(n_pipe, n_head, *refs),
        out_shape=[jax.ShapeDtypeStruct(shape, keys.dtype)] * 2,
        in_specs=[whole, whole],
        out_specs=[pl.BlockSpec(memory_space=pl.ANY)] * 2,
        scratch_shapes=[
            pltpu.VMEM(shape, keys.dtype),
            pltpu.VMEM(shape, keys.dtype),
            dma((2,)),
            dma((2, n_head)),
            dma((2, n_head)),
            dma((2, n_pipe)),
            dma((2, n_pipe)),
            dma((2, n_pipe)),
            dma((2, n_pipe)),
            dma((2, n_pipe)),
        ],
        compiler_params=pltpu.CompilerParams(collective_id=0, has_side_effects=True, vmem_limit_bytes=60 * 2 ** 20),
        name="gather",
    )(keys, values)


def on_device(sizes, queries, keys, values, slice_index):
    key_all, value_all = gather(keys, values, *sizes)
    index = lax.dynamic_index_in_dim(slice_index, lax.axis_index("pipe"), axis=1, keepdims=False)
    return attend(queries, key_all, value_all, index)


def solution(mesh):
    sizes = (mesh.shape["pipe"], mesh.shape["head"])
    return jax.shard_map(
        lambda *arrays: on_device(sizes, *arrays),
        mesh=mesh,
        in_specs=(
            P(None, "pipe", "head"),
            P(("pipe", "head"), None),
            P(("pipe", "head"), None),
            P(),
        ),
        out_specs=P(None, "pipe", "head"),
        check_vma=False,
    )
```

```python
import math

import jax
import jax.numpy as jnp
from jax import lax
from jax.experimental import pallas as pl
from jax.experimental.pallas import tpu as pltpu
from jax.sharding import PartitionSpec as P

HEAD_SIZE = 128
NEG = -1e30
TO_EXP2 = HEAD_SIZE ** (-0.5) * math.log2(math.e)
PAIRS = 2
UNROLL = 4


def scores_of(query, key_block):
    return lax.dot_general(query, key_block, (((1,), (1,)), ((), ())), preferred_element_type=jnp.float32)


def weigh(scores, peak, value_block):
    weights = jnp.exp2((scores - peak) * TO_EXP2).astype(jnp.bfloat16)
    ones = jnp.ones(value_block.shape, jnp.bfloat16)
    return jnp.dot(weights, jnp.concatenate([value_block, ones], axis=1), preferred_element_type=jnp.float32)


MESH = pl.DeviceIdType.MESH


def fused_kernel(n_pipe, n_head, index_ref, q_ref, k_ref, v_ref, o_ref, kbuf, vbuf, qbuf, obuf, best_ref, accum_ref, local_sem, head_send, head_recv, left_send, right_send, side_send, chunk_recv, q_sem, out_sem):
    me = lax.axis_index("pipe")
    head = lax.axis_index("head")
    side = me + 1 - 2 * lax.rem(me, 2)
    row = lax.div(me, 2)
    line = n_pipe // 2
    has_left, has_right = row > 0, row < line - 1
    piece = k_ref.shape[0]
    rows = piece * n_head
    width = kbuf.shape[1]
    ins, bufs = (k_ref, v_ref), (kbuf, vbuf)

    barrier = pltpu.get_barrier_semaphore()
    for other in range(1, n_head):
        pl.semaphore_signal(barrier, inc=1, device_id=(me, lax.rem(head + other, n_head)), device_id_type=MESH)
    pl.semaphore_signal(barrier, inc=1, device_id=(side, head), device_id_type=MESH)

    @pl.when(has_left)
    def _():
        pl.semaphore_signal(barrier, inc=1, device_id=(me - 2, head), device_id_type=MESH)

    @pl.when(has_right)
    def _():
        pl.semaphore_signal(barrier, inc=1, device_id=(me + 2, head), device_id_type=MESH)

    pl.semaphore_wait(barrier, n_head + jnp.where(has_left, 1, 0) + jnp.where(has_right, 1, 0))

    def chunk(kind, owner):
        return bufs[kind].at[pl.ds(pl.multiple_of(owner * rows, rows), rows), :]

    def spot(kind, source):
        return bufs[kind].at[pl.ds(pl.multiple_of(me * rows + source * piece, piece), piece), :]

    def columns(kind, target):
        return ins[kind].at[:, pl.ds(pl.multiple_of(target * width, width), width)]

    def exchange(kind, other):
        return pltpu.make_async_remote_copy(
            columns(kind, lax.rem(head + other, n_head)), spot(kind, head),
            head_send.at[kind, other], head_recv.at[kind, other],
            device_id=(me, lax.rem(head + other, n_head)), device_id_type=MESH)

    def arrival(kind, other):
        source = lax.rem(head + n_head - other, n_head)
        return pltpu.make_async_remote_copy(
            columns(kind, head), spot(kind, source),
            head_send.at[kind, other], head_recv.at[kind, other],
            device_id=(me, source), device_id_type=MESH)

    def pass_on(kind, owner, target, sems):
        return pltpu.make_async_remote_copy(
            chunk(kind, owner), chunk(kind, owner), sems.at[kind, owner], chunk_recv.at[kind, owner],
            device_id=(target, head), device_id_type=MESH)

    def to_left(kind, owner):
        return pass_on(kind, owner, me - 2, left_send)

    def to_right(kind, owner):
        return pass_on(kind, owner, me + 2, right_send)

    def to_side(kind, owner):
        return pass_on(kind, owner, side, side_send)

    for kind in range(2):
        for other in range(1, n_head):
            exchange(kind, other).start()
        pltpu.make_async_copy(columns(kind, head), spot(kind, head), local_sem.at[kind]).start()
    pltpu.make_async_copy(q_ref, qbuf, q_sem).start()
    for kind in range(2):
        pltpu.make_async_copy(columns(kind, head), spot(kind, head), local_sem.at[kind]).wait()
        for other in range(1, n_head):
            arrival(kind, other).wait_recv()
        to_side(kind, me).start()

        @pl.when(has_left)
        def _():
            to_left(kind, me).start()

        @pl.when(has_right)
        def _():
            to_right(kind, me).start()

    def handle(step):
        for kind in range(2):

            @pl.when(row >= step)
            def _():
                owner = me - 2 * step
                to_right(kind, owner).wait_recv()
                to_side(kind, owner).start()

                @pl.when(has_right)
                def _():
                    to_right(kind, owner).start()

            @pl.when(row + step < line)
            def _():
                owner = me + 2 * step
                to_left(kind, owner).wait_recv()
                to_side(kind, owner).start()

                @pl.when(has_left)
                def _():
                    to_left(kind, owner).start()

    ticks, _, q_width = qbuf.shape
    heads = width // HEAD_SIZE
    group = q_width // width
    batches = group // UNROLL
    strip = UNROLL * HEAD_SIZE
    bodies = ticks * heads * batches
    pair_rows = 2 * rows
    steps = line // PAIRS
    diff = lax.broadcasted_iota(jnp.int32, (rows, pair_rows), 1) - lax.broadcasted_iota(jnp.int32, (rows, pair_rows), 0)
    reach = jnp.minimum(row, line - 1 - row)

    def nearest(place):
        offset = lax.div(place + 1, 2)
        near = jnp.where(lax.rem(place, 2) == 1, row - offset, row + offset)
        far = jnp.where(row < line - 1 - row, place, line - 1 - place)
        return jnp.where(place <= 2 * reach, near, far)

    def strip_out(item):
        tick = lax.div(item, heads * batches)
        at = pl.ds(pl.multiple_of(lax.rem(item, heads * batches) * strip, strip), strip)
        return pltpu.make_async_copy(obuf.at[tick, :, at], o_ref.at[tick, :, at], out_sem.at[item])

    def wide(array, count):
        return jnp.concatenate([array] * count, axis=1)

    def compute(step, first, last):
        pairs = [nearest(step * PAIRS + at) for at in range(PAIRS)]
        for pair in pairs:
            for kind in range(2):
                to_side(kind, 2 * pair + lax.rem(side, 2)).wait_recv()
        spans = [pl.ds(pl.multiple_of(pair * pair_rows, pair_rows), pair_rows) for pair in pairs]

        @pl.loop(0, bodies)
        def _(item):
            if not last:
                for at in range(PAIRS):
                    later = (step + 1) * PAIRS + at

                    @pl.when(item == (1 + 3 * at) * bodies // 8)
                    def _():
                        handle(later)

            tick = lax.div(item, heads * batches)
            strip_at = lax.rem(item, heads * batches)
            kv = pl.ds(pl.multiple_of(lax.div(strip_at, batches) * HEAD_SIZE, HEAD_SIZE), HEAD_SIZE)
            start = index_ref[tick, me] * rows
            for u in range(UNROLL):
                at = pl.ds(pl.multiple_of(strip_at * strip + u * HEAD_SIZE, HEAD_SIZE), HEAD_SIZE)
                slot = item * UNROLL + u
                query = qbuf[tick, :, at]
                scores = jnp.concatenate([
                    jnp.where(diff <= start - pair * pair_rows, scores_of(query, kbuf[span, kv]), NEG)
                    for pair, span in zip(pairs, spans)
                ], axis=1)
                top = jnp.broadcast_to(jnp.max(scores, axis=-1, keepdims=True), (rows, HEAD_SIZE))
                if first:
                    peak = top
                else:
                    before = best_ref[slot]
                    peak = jnp.maximum(before, top)
                block = jnp.concatenate([vbuf[span, kv] for span in spans], axis=0)
                result = weigh(scores, wide(peak, PAIRS * pair_rows // HEAD_SIZE), block)
                if not first:
                    result = result + accum_ref[slot] * wide(jnp.exp2((before - peak) * TO_EXP2), 2)
                if last:
                    obuf[tick, :, at] = (result[:, :HEAD_SIZE] / result[:, HEAD_SIZE:]).astype(obuf.dtype)
                else:
                    best_ref[slot] = peak
                    accum_ref[slot] = result
            if last:
                strip_out(item).start()

    handle(1)
    pltpu.make_async_copy(q_ref, qbuf, q_sem).wait()
    compute(0, True, steps == 1)
    if steps > 2:

        @pl.loop(1, steps - 1)
        def _(step):
            compute(step, False, False)

    if steps > 1:
        compute(steps - 1, False, True)

    for kind in range(2):
        for other in range(1, n_head):
            exchange(kind, other).wait_send()

    @pl.loop(0, line)
    def _(index):
        for kind in range(2):
            owner = 2 * index + lax.rem(me, 2)
            to_side(kind, owner).wait_send()

            @pl.when(jnp.logical_and(has_right, index <= row))
            def _():
                to_right(kind, owner).wait_send()

            @pl.when(jnp.logical_and(has_left, index >= row))
            def _():
                to_left(kind, owner).wait_send()

    @pl.loop(0, bodies)
    def _(item):
        strip_out(item).wait()


def on_device(sizes, queries, keys, values, slice_index):
    n_pipe, n_head = sizes
    ticks, rows, columns = queries.shape
    shape = (rows * n_pipe, keys.shape[1] // n_head)
    slots = ticks * columns // HEAD_SIZE
    whole = pl.BlockSpec(memory_space=pltpu.VMEM)
    anywhere = pl.BlockSpec(memory_space=pl.ANY)
    dma = pltpu.SemaphoreType.DMA
    return pl.pallas_call(
        lambda *refs: fused_kernel(n_pipe, n_head, *refs),
        out_shape=jax.ShapeDtypeStruct(queries.shape, queries.dtype),
        in_specs=[pl.BlockSpec(memory_space=pltpu.SMEM), anywhere, whole, whole],
        out_specs=anywhere,
        scratch_shapes=[
            pltpu.VMEM(shape, keys.dtype),
            pltpu.VMEM(shape, keys.dtype),
            pltpu.VMEM(queries.shape, queries.dtype),
            pltpu.VMEM(queries.shape, queries.dtype),
            pltpu.VMEM((slots, rows, HEAD_SIZE), jnp.float32),
            pltpu.VMEM((slots, rows, 2 * HEAD_SIZE), jnp.float32),
            dma((2,)),
            dma((2, n_head)),
            dma((2, n_head)),
            dma((2, n_pipe)),
            dma((2, n_pipe)),
            dma((2, n_pipe)),
            dma((2, n_pipe)),
            dma,
            dma((slots // UNROLL,)),
        ],
        compiler_params=pltpu.CompilerParams(collective_id=0, has_side_effects=True, vmem_limit_bytes=60 * 2 ** 20),
        name="fused",
    )(slice_index, queries, keys, values)


def solution(mesh):
    sizes = (mesh.shape["pipe"], mesh.shape["head"])
    return jax.shard_map(
        lambda *arrays: on_device(sizes, *arrays),
        mesh=mesh,
        in_specs=(
            P(None, "pipe", "head"),
            P(("pipe", "head"), None),
            P(("pipe", "head"), None),
            P(),
        ),
        out_specs=P(None, "pipe", "head"),
        check_vma=False,
    )
```

```python
import math

import jax
import jax.numpy as jnp
from jax import lax
from jax.experimental import pallas as pl
from jax.experimental.pallas import tpu as pltpu
from jax.sharding import PartitionSpec as P

HEAD_SIZE = 128
NEG = -1e30
TO_EXP2 = HEAD_SIZE ** (-0.5) * math.log2(math.e)
PAIRS = 2
UNROLL = 8


def scores_of(query, key_block):
    return lax.dot_general(query, key_block, (((1,), (1,)), ((), ())), preferred_element_type=jnp.float32)


def weigh(scores, peak, value_block):
    weights = jnp.exp2((scores - peak) * TO_EXP2).astype(jnp.bfloat16)
    ones = jnp.ones(value_block.shape, jnp.bfloat16)
    return jnp.dot(weights, jnp.concatenate([value_block, ones], axis=1), preferred_element_type=jnp.float32)


MESH = pl.DeviceIdType.MESH


def fused_kernel(n_pipe, n_head, index_ref, q_ref, k_ref, v_ref, o_ref, kbuf, vbuf, qbuf, obuf, best_ref, accum_ref, local_sem, head_send, head_recv, left_send, right_send, side_send, chunk_recv, q_sem, out_sem):
    me = lax.axis_index("pipe")
    head = lax.axis_index("head")
    side = me + 1 - 2 * lax.rem(me, 2)
    row = lax.div(me, 2)
    line = n_pipe // 2
    has_left, has_right = row > 0, row < line - 1
    piece = k_ref.shape[0]
    rows = piece * n_head
    width = kbuf.shape[1]
    ins, bufs = (k_ref, v_ref), (kbuf, vbuf)

    barrier = pltpu.get_barrier_semaphore()
    for other in range(1, n_head):
        pl.semaphore_signal(barrier, inc=1, device_id=(me, lax.rem(head + other, n_head)), device_id_type=MESH)
    pl.semaphore_signal(barrier, inc=1, device_id=(side, head), device_id_type=MESH)

    @pl.when(has_left)
    def _():
        pl.semaphore_signal(barrier, inc=1, device_id=(me - 2, head), device_id_type=MESH)

    @pl.when(has_right)
    def _():
        pl.semaphore_signal(barrier, inc=1, device_id=(me + 2, head), device_id_type=MESH)

    pl.semaphore_wait(barrier, n_head + jnp.where(has_left, 1, 0) + jnp.where(has_right, 1, 0))

    def chunk(kind, owner):
        return bufs[kind].at[pl.ds(pl.multiple_of(owner * rows, rows), rows), :]

    def spot(kind, source):
        return bufs[kind].at[pl.ds(pl.multiple_of(me * rows + source * piece, piece), piece), :]

    def columns(kind, target):
        return ins[kind].at[:, pl.ds(pl.multiple_of(target * width, width), width)]

    def exchange(kind, other):
        return pltpu.make_async_remote_copy(
            columns(kind, lax.rem(head + other, n_head)), spot(kind, head),
            head_send.at[kind, other], head_recv.at[kind, other],
            device_id=(me, lax.rem(head + other, n_head)), device_id_type=MESH)

    def arrival(kind, other):
        source = lax.rem(head + n_head - other, n_head)
        return pltpu.make_async_remote_copy(
            columns(kind, head), spot(kind, source),
            head_send.at[kind, other], head_recv.at[kind, other],
            device_id=(me, source), device_id_type=MESH)

    def pass_on(kind, owner, target, sems):
        return pltpu.make_async_remote_copy(
            chunk(kind, owner), chunk(kind, owner), sems.at[kind, owner], chunk_recv.at[kind, owner],
            device_id=(target, head), device_id_type=MESH)

    def to_left(kind, owner):
        return pass_on(kind, owner, me - 2, left_send)

    def to_right(kind, owner):
        return pass_on(kind, owner, me + 2, right_send)

    def to_side(kind, owner):
        return pass_on(kind, owner, side, side_send)

    for kind in range(2):
        for other in range(1, n_head):
            exchange(kind, other).start()
        pltpu.make_async_copy(columns(kind, head), spot(kind, head), local_sem.at[kind]).start()
    pltpu.make_async_copy(q_ref, qbuf, q_sem).start()
    for kind in range(2):
        pltpu.make_async_copy(columns(kind, head), spot(kind, head), local_sem.at[kind]).wait()
        for other in range(1, n_head):
            arrival(kind, other).wait_recv()
        to_side(kind, me).start()

        @pl.when(has_left)
        def _():
            to_left(kind, me).start()

        @pl.when(has_right)
        def _():
            to_right(kind, me).start()

    def handle(step):
        for kind in range(2):

            @pl.when(row >= step)
            def _():
                owner = me - 2 * step
                to_right(kind, owner).wait_recv()
                to_side(kind, owner).start()

                @pl.when(has_right)
                def _():
                    to_right(kind, owner).start()

            @pl.when(row + step < line)
            def _():
                owner = me + 2 * step
                to_left(kind, owner).wait_recv()
                to_side(kind, owner).start()

                @pl.when(has_left)
                def _():
                    to_left(kind, owner).start()

    ticks, _, q_width = qbuf.shape
    heads = width // HEAD_SIZE
    group = q_width // width
    batches = group // UNROLL
    strip = UNROLL * HEAD_SIZE
    bodies = ticks * heads * batches
    pair_rows = 2 * rows
    steps = line // PAIRS
    diff = lax.broadcasted_iota(jnp.int32, (rows, pair_rows), 1) - lax.broadcasted_iota(jnp.int32, (rows, pair_rows), 0)
    reach = jnp.minimum(row, line - 1 - row)

    def nearest(place):
        offset = lax.div(place + 1, 2)
        near = jnp.where(lax.rem(place, 2) == 1, row - offset, row + offset)
        far = jnp.where(row < line - 1 - row, place, line - 1 - place)
        return jnp.where(place <= 2 * reach, near, far)

    def strip_out(item):
        tick = lax.div(item, heads * batches)
        at = pl.ds(pl.multiple_of(lax.rem(item, heads * batches) * strip, strip), strip)
        return pltpu.make_async_copy(obuf.at[tick, :, at], o_ref.at[tick, :, at], out_sem.at[item])

    def wide(array, count):
        return jnp.concatenate([array] * count, axis=1)

    def compute(step, first, last):
        pairs = [nearest(step * PAIRS + at) for at in range(PAIRS)]
        for pair in pairs:
            for kind in range(2):
                to_side(kind, 2 * pair + lax.rem(side, 2)).wait_recv()
        spans = [pl.ds(pl.multiple_of(pair * pair_rows, pair_rows), pair_rows) for pair in pairs]

        @pl.loop(0, bodies)
        def _(item):
            if not last:
                for at in range(PAIRS):
                    later = (step + 1) * PAIRS + at

                    @pl.when(item == (1 + 3 * at) * bodies // 8)
                    def _():
                        handle(later)

            tick = lax.div(item, heads * batches)
            strip_at = lax.rem(item, heads * batches)
            kv = pl.ds(pl.multiple_of(lax.div(strip_at, batches) * HEAD_SIZE, HEAD_SIZE), HEAD_SIZE)
            start = index_ref[tick, me] * rows
            for u in range(UNROLL):
                at = pl.ds(pl.multiple_of(strip_at * strip + u * HEAD_SIZE, HEAD_SIZE), HEAD_SIZE)
                slot = item * UNROLL + u
                query = qbuf[tick, :, at]
                scores = jnp.concatenate([
                    jnp.where(diff <= start - pair * pair_rows, scores_of(query, kbuf[span, kv]), NEG)
                    for pair, span in zip(pairs, spans)
                ], axis=1)
                top = jnp.broadcast_to(jnp.max(scores, axis=-1, keepdims=True), (rows, HEAD_SIZE))
                if first:
                    peak = top
                else:
                    before = best_ref[slot]
                    peak = jnp.maximum(before, top)
                block = jnp.concatenate([vbuf[span, kv] for span in spans], axis=0)
                result = weigh(scores, wide(peak, PAIRS * pair_rows // HEAD_SIZE), block)
                if not first:
                    result = result + accum_ref[slot] * wide(jnp.exp2((before - peak) * TO_EXP2), 2)
                if last:
                    obuf[tick, :, at] = (result[:, :HEAD_SIZE] / result[:, HEAD_SIZE:]).astype(obuf.dtype)
                else:
                    best_ref[slot] = peak
                    accum_ref[slot] = result
            if last:
                strip_out(item).start()

    handle(1)
    pltpu.make_async_copy(q_ref, qbuf, q_sem).wait()
    compute(0, True, steps == 1)
    if steps > 2:

        @pl.loop(1, steps - 1)
        def _(step):
            compute(step, False, False)

    if steps > 1:
        compute(steps - 1, False, True)

    for kind in range(2):
        for other in range(1, n_head):
            exchange(kind, other).wait_send()

    @pl.loop(0, line)
    def _(index):
        for kind in range(2):
            owner = 2 * index + lax.rem(me, 2)
            to_side(kind, owner).wait_send()

            @pl.when(jnp.logical_and(has_right, index <= row))
            def _():
                to_right(kind, owner).wait_send()

            @pl.when(jnp.logical_and(has_left, index >= row))
            def _():
                to_left(kind, owner).wait_send()

    @pl.loop(0, bodies)
    def _(item):
        strip_out(item).wait()


def on_device(sizes, queries, keys, values, slice_index):
    n_pipe, n_head = sizes
    ticks, rows, columns = queries.shape
    shape = (rows * n_pipe, keys.shape[1] // n_head)
    slots = ticks * columns // HEAD_SIZE
    whole = pl.BlockSpec(memory_space=pltpu.VMEM)
    anywhere = pl.BlockSpec(memory_space=pl.ANY)
    dma = pltpu.SemaphoreType.DMA
    return pl.pallas_call(
        lambda *refs: fused_kernel(n_pipe, n_head, *refs),
        out_shape=jax.ShapeDtypeStruct(queries.shape, queries.dtype),
        in_specs=[pl.BlockSpec(memory_space=pltpu.SMEM), anywhere, whole, whole],
        out_specs=anywhere,
        scratch_shapes=[
            pltpu.VMEM(shape, keys.dtype),
            pltpu.VMEM(shape, keys.dtype),
            pltpu.VMEM(queries.shape, queries.dtype),
            pltpu.VMEM(queries.shape, queries.dtype),
            pltpu.VMEM((slots, rows, HEAD_SIZE), jnp.float32),
            pltpu.VMEM((slots, rows, 2 * HEAD_SIZE), jnp.float32),
            dma((2,)),
            dma((2, n_head)),
            dma((2, n_head)),
            dma((2, n_pipe)),
            dma((2, n_pipe)),
            dma((2, n_pipe)),
            dma((2, n_pipe)),
            dma,
            dma((slots // UNROLL,)),
        ],
        compiler_params=pltpu.CompilerParams(collective_id=0, has_side_effects=True, vmem_limit_bytes=60 * 2 ** 20),
        name="fused",
    )(slice_index, queries, keys, values)


def solution(mesh):
    sizes = (mesh.shape["pipe"], mesh.shape["head"])
    return jax.shard_map(
        lambda *arrays: on_device(sizes, *arrays),
        mesh=mesh,
        in_specs=(
            P(None, "pipe", "head"),
            P(("pipe", "head"), None),
            P(("pipe", "head"), None),
            P(),
        ),
        out_specs=P(None, "pipe", "head"),
        check_vma=False,
    )
```
